256 devices in a mesh: rows: 4 (over z_hi), cols: 64 (over y, z_lo, x, core).
Axes of the slice: x: 4, y: 4, z: 8 (z_hi: 4, z_lo: 2; z = z_hi * 2 + z_lo), core: 2. Of those that a mesh axis runs over, the one named last changes fastest.
Arguments:
- slab: bfloat16 [8192, 65536], P('rows', 'cols'), may hold values from -6 to 6
- transforms: bfloat16 [64, 16384, 512], P('cols', 'rows'), may hold values from -0.25 to 0.25
- owners: int32 [2, 4], replicated, may hold values from 0 to 63, as said below
Outputs:
- updated: bfloat16 [8192, 65536], P('rows', 'cols')
The draws below stay inside these ranges and needn't reach their ends.
Inputs may be any that keep to these rules, and one draw needn't show every extreme that they name: For each row block, the owners of different rounds differ.
All inputs are finite; a program needn't handle non-finite values.
Results may differ from the reference program's by a relative error of at most 0.0063.
Values may be sent and summed in bfloat16 or wider, within the bound.
A program may use at most 64 MiB of HBM per device.

```python
import jax
import jax.numpy as jnp
from jax import lax

W = 512
ROUNDS = 2
WINS = 4
STAGGER = 256
SLAB_ROWS = 8192
SLAB_COLS = 65536
POOL_ROWS = 16384
N_ROWS = 4
N_COLS = 64


def place_value(shuffled, value, position):
    found = jnp.argmax(shuffled == value)
    displaced = shuffled[position]
    return shuffled.at[found].set(displaced).at[position].set(value)


def draw_owners(key, part):
    base = jax.random.fold_in(key, 11)
    key_list = jax.random.split(base, N_ROWS + 4)
    shuffled = jnp.stack([jax.random.permutation(key_list[index], N_COLS) for index in range(N_ROWS)]).astype(jnp.int32)
    top_row = jax.random.randint(key_list[N_ROWS], (), 0, N_ROWS)
    low_row = (top_row + jax.random.randint(key_list[N_ROWS + 1], (), 1, N_ROWS)) % N_ROWS
    top_pos = jax.random.randint(key_list[N_ROWS + 2], (), 0, ROUNDS)
    low_pos = jax.random.randint(key_list[N_ROWS + 3], (), 0, ROUNDS)
    block_ids = jnp.arange(N_ROWS)[:, None]
    with_top = jax.vmap(lambda vector: place_value(vector, N_COLS - 1, top_pos))(shuffled)
    shuffled = jnp.where(block_ids == top_row, with_top, shuffled)
    with_low = jax.vmap(lambda vector: place_value(vector, 0, low_pos))(shuffled)
    shuffled = jnp.where(block_ids == low_row, with_low, shuffled)
    return shuffled[:, :ROUNDS].T.astype(jnp.int32)


def level_of(key, shape, cuts, low, high):
    loudness, own = 1.0, jax.random.fold_in(key, 6)
    for dim, shards_of in cuts:
        steps = jnp.exp(jax.random.uniform(jax.random.fold_in(own, dim), (shards_of,), jnp.float32, low / len(cuts), high / len(cuts)))
        loudness = loudness * jnp.repeat(steps, shape[dim] // shards_of).reshape([-1 if axis == dim else 1 for axis in range(len(shape))])
    return loudness


def centred(stream_key, dims, scale, bound, cuts=(), dtype=jnp.bfloat16):
    values = scale * jax.random.normal(stream_key, dims, jnp.float32)
    if cuts:
        values = values * level_of(stream_key, dims, cuts, -0.22, 0.18)
    return jnp.clip(values, -bound, bound).astype(dtype)


def setup_inputs(seed: int = 0) -> dict:
    key_of = jax.random.split(jax.random.key(seed), 4)
    return {
        "slab": centred(key_of[0], (SLAB_ROWS, SLAB_COLS), 1.0, 6.0, ((0, 4), (1, 64))),
        "transforms": centred(key_of[1], (N_COLS, POOL_ROWS, W), W ** -0.5, 0.25, ((0, 64), (1, 4))),
        "owners": draw_owners(jax.random.fold_in(key_of[3], 71), 0),
    }


def apply_pair(operands):
    transform, block_rows = operands
    product = lax.dot_general(transform, block_rows, (((0,), (0,)), ((), ())), preferred_element_type=jnp.float32)
    return product.astype(jnp.bfloat16)


def reference(slab, transforms, owners):
    span_rows = 2 * WINS * W
    total_windows = N_ROWS * WINS
    matrix = slab
    slab_width = slab.shape[1]
    for round_index in range(ROUNDS):
        pieces = []
        for row_block in range(N_ROWS):
            chosen = lax.dynamic_index_in_dim(transforms, owners[round_index, row_block].astype(jnp.int32), 0, keepdims=False)
            pieces.append(chosen[row_block * span_rows:(row_block + 1) * span_rows].reshape(2, WINS, W, W))
        stacked = jnp.stack(pieces)
        set_one = stacked[:, 0].reshape(total_windows, W, W)
        set_two = stacked[:, 1].reshape(total_windows, W, W)[:total_windows - 1]
        windows = matrix.reshape(total_windows, W, slab_width)
        matrix = lax.map(apply_pair, (set_one, windows)).reshape(matrix.shape)
        finish = STAGGER + (total_windows - 1) * W
        middle = matrix[STAGGER:finish].reshape(total_windows - 1, W, slab_width)
        middle = lax.map(apply_pair, (set_two, middle)).reshape(-1, slab_width)
        matrix = jnp.concatenate([matrix[:STAGGER], middle, matrix[finish:]], 0)
    return matrix
```

```python
import functools

import jax
import jax.numpy as jnp
from jax import lax
from jax.experimental import pallas as pl
from jax.experimental.pallas import tpu as pltpu
from jax.sharding import PartitionSpec as P

MESH = pl.DeviceIdType.MESH

PARENT = (
    0, 10234, 10234, 10324, 21034, 40231, 40231, 4321,
    10324, 43102, 40123, 34201, 1423, 30421, 30412, 13042,
    10324, 30124, 42310, 31240, 1342, 21043, 24301, 43102,
    1324, 24310, 42130, 21034, 13042, 40213, 20314, 12430,
)
DEPTH = (
    11111, 13333, 22464, 31555, 53531, 24442, 33553, 62664,
    55133, 44266, 55355, 44646, 44242, 35353, 44466, 53355,
    66224, 55335, 64446, 55555, 55333, 46644, 55555, 64644,
    35313, 26426, 53555, 44464, 66622, 35535, 44646, 53553,
)
OPPOSITE = (1, 0, 3, 2, 4)
LINKS = 5
LAG = 5
CHUNKS = 128
SEQS = 26
STEPS = SEQS + LAG * 5
G = 16
BANDS = 8
BAND = 128
W = 512
EDGE = 256
EARLY = 3 + LAG * 5


def digits(words):
    return [[word // 10 ** (4 - i) % 10 for i in range(5)] for word in words]


def tree_tables():
    parent = digits(PARENT)
    depth = digits(DEPTH)
    forward = []
    for place in range(32):
        y, z, x = place // 8, place // 4 % 2, place % 4
        ahead = (
            (y * 2 + z) * 4 + (x + 1) % 4,
            (y * 2 + z) * 4 + (x + 3) % 4,
            ((y + 1) % 4 * 2 + z) * 4 + x,
            ((y + 3) % 4 * 2 + z) * 4 + x,
            (y * 2 + 1 - z) * 4 + x,
        )
        row = []
        for link in range(LINKS):
            source = 0
            if place and ahead[link]:
                tree = parent[ahead[link]].index(OPPOSITE[link])
                source = parent[place][tree]
            row.append(source)
        forward.append(row)
    flat = []
    for place in range(32):
        flat += forward[place] + parent[place] + [level - 1 for level in depth[place]]
    return jnp.array(flat, jnp.int32)


def sweep_kernel(
    owners, table, slot_hbm, slab_hbm, out_hbm,
    own, other, recv, mirror, stage, q, w, below, top, back,
    load_sem, part_send, part_recv, send_sem, recv_sem, mirror_send, mirror_recv,
    up_send, up_recv, down_send, down_recv, out_sem,
):
    row = lax.axis_index("rows")
    col = lax.axis_index("cols")
    core = col % 2
    x = (col // 2) % 4
    z = (col // 8) % 2
    y = col // 16

    def device(yy, zz, xx, cc):
        return {"cols": ((yy * 2 + zz) * 4 + xx) * 2 + cc}

    peers = (
        device(y, z, (x + 1) % 4, core),
        device(y, z, (x + 3) % 4, core),
        device((y + 1) % 4, z, x, core),
        device((y + 3) % 4, z, x, core),
        device(y, 1 - z, x, core),
    )
    partner = device(y, z, x, 1 - core)
    upper = {"rows": (row + 3) % 4}
    lower = {"rows": (row + 1) % 4}

    load = pltpu.make_async_copy(slot_hbm, own, load_sem.at[0])
    load.start()
    load_slab = pltpu.make_async_copy(slab_hbm, w, load_sem.at[1])
    load_slab.start()
    barrier = pltpu.get_barrier_semaphore()
    for peer in peers + (partner, upper, lower):
        pl.semaphore_signal(barrier, inc=1, device_id=peer, device_id_type=MESH)
    pl.semaphore_wait(barrier, 8)

    def part(index, first, count, half):
        return pltpu.make_async_remote_copy(
            src_ref=slot_hbm.at[pl.ds(first, count), half],
            dst_ref=other.at[pl.ds(first, count), half],
            send_sem=part_send.at[index],
            recv_sem=part_recv.at[index],
            device_id=partner,
            device_id_type=MESH,
        )

    parts = (part(0, 0, 32, 1 - core), part(1, 32, 96, 1 - core), part(2, 0, 128, core))
    for copy in parts:
        copy.start()

    place, rooted, root_core = [], [], []
    for k in range(2):
        owner = owners[k, row]
        oy, oz, ox, oc = owner // 16, (owner // 8) % 2, (owner // 2) % 4, owner % 2
        where = (((y + 4 - oy) % 4) * 2 + (z + 2 - oz) % 2) * 4 + (x + 4 - ox) % 4
        place.append(where)
        rooted.append(where == 0)
        root_core.append(oc == core)
    source = [[table[place[k] * 15 + l] for l in range(LINKS)] for k in range(2)]
    entry = [[table[place[k] * 15 + 5 + l] for l in range(LINKS)] for k in range(2)]
    level = [[table[place[k] * 15 + 10 + l] for l in range(LINKS)] for k in range(2)]

    def fill(step, local, passed):
        for l in range(LINKS):
            chunk = None
            if local:
                chunk = step * LINKS + l
                if isinstance(chunk, int):
                    chunk = min(chunk, CHUNKS - 1)
                mine, theirs = own[chunk, core], other[chunk, core]
            for k in range(2):
                value = None
                if passed:
                    value = recv[step - LAG, 0, k]
                    for m in range(1, LINKS):
                        value = jnp.where(source[k][l] == m, recv[step - LAG, m, k], value)
                if local:
                    first = jnp.where(root_core[k], mine, theirs)
                    value = first if value is None else jnp.where(rooted[k], first, value)
                stage[step, l, k] = value

    def send(step):
        for l in range(LINKS):
            pltpu.make_async_remote_copy(
                src_ref=stage.at[step, l],
                dst_ref=recv.at[step, OPPOSITE[l]],
                send_sem=send_sem.at[step],
                recv_sem=recv_sem.at[step],
                device_id=peers[l],
                device_id_type=MESH,
            ).start()

    def whole(ref, step, sem):
        return pltpu.make_async_copy(ref.at[step], ref.at[step], sem.at[step])

    def reflect(step):
        return pltpu.make_async_remote_copy(
            src_ref=recv.at[step],
            dst_ref=mirror.at[step],
            send_sem=mirror_send.at[step],
            recv_sem=mirror_recv.at[step],
            device_id=partner,
            device_id_type=MESH,
        )

    def arrive(step):
        whole(recv, step, recv_sem).wait()
        reflect(step).start()

    def pass_on(step, carry):
        arrive(step - LAG)
        fill(step, False, True)
        send(step)
        return carry

    def both(step, carry):
        arrive(step - LAG)
        fill(step, True, True)
        send(step)
        return carry

    def reflected(step, carry):
        reflect(step).wait_recv()
        return carry

    load.wait()
    parts[0].wait_recv()
    for step in range(LAG):
        fill(step, True, False)
        send(step)
    parts[1].wait_recv()
    lax.fori_loop(LAG, SEQS - 1, both, 0)
    both(SEQS - 1, 0)
    lax.fori_loop(SEQS, EARLY + LAG + 3, pass_on, 0)
    parts[2].wait_recv()
    lax.fori_loop(0, EARLY + 1, reflected, 0)

    def local_rows(k, chunk, half):
        return jnp.where(root_core[k], own[chunk, half], other[chunk, half])

    for chunk in range(W // (2 * G)):
        step, t = chunk // LINKS, chunk % LINKS
        for half, got in ((core, recv), (1 - core, mirror)):
            value = got[step, 0, 0]
            for d in range(6):
                here = got[step + LAG * d, 0, 0]
                for m in range(1, LINKS):
                    here = jnp.where(entry[0][t] == m, got[step + LAG * d, m, 0], here)
                value = jnp.where(level[0][t] == d, here, value)
            q[0, chunk, half] = jnp.where(rooted[0], local_rows(0, chunk, half), value)

    def matrix(k, window):
        return q[k, window * G : (window + 1) * G].reshape(W, W)

    def turn(k, window):
        turned = matrix(k, window).T
        q[k, window * G : (window + 1) * G] = turned.reshape(G, 2, G, W)

    def product(left, right):
        return jnp.dot(left, right, preferred_element_type=jnp.float32).astype(jnp.bfloat16)

    def full(k, window, first):
        def panel(index, carry):
            columns = pl.ds(pl.multiple_of(index * 256, 256), 256)
            rows = pl.ds(first, W)
            w[rows, columns] = product(matrix(k, window), w[rows, columns])
            return carry

        lax.fori_loop(0, 4, panel, 0)

    def band(c):
        return pl.ds(c * BAND, BAND)

    def up(k, c):
        return pltpu.make_async_remote_copy(
            src_ref=w.at[pl.ds(0, EDGE), band(c)],
            dst_ref=below.at[k, :, band(c)],
            send_sem=up_send.at[k, c],
            recv_sem=up_recv.at[k, c],
            device_id=upper,
            device_id_type=MESH,
        )

    def down(k, c):
        return pltpu.make_async_remote_copy(
            src_ref=back.at[k, :, band(c)],
            dst_ref=top.at[k, :, band(c)],
            send_sem=down_send.at[k, c],
            recv_sem=down_recv.at[k, c],
            device_id=lower,
            device_id_type=MESH,
        )

    inner = row > 0
    outer = row < 3

    load_slab.wait()
    turn(0, 0)
    full(0, 0, 0)

    @pl.when(row == 0)
    def _():
        top[0] = w[0:EDGE, :]

    lax.fori_loop(EARLY + LAG + 3, STEPS, pass_on, 0)

    @pl.when(inner)
    def _():
        for c in range(BANDS):
            up(0, c).start()

    def drain(step, carry):
        arrive(step)
        return carry

    lax.fori_loop(STEPS - LAG, STEPS, drain, 0)
    lax.fori_loop(EARLY + 1, STEPS, reflected, 0)

    def place_chunk(k, t, step):
        chunk = step * LINKS + t
        index = level[k][t] * LAG + step
        for half, got in ((core, recv), (1 - core, mirror)):
            q[k, chunk, half] = jnp.where(
                rooted[k], local_rows(k, chunk, half), got[index, entry[k][t], k]
            )

    def gather(k, first):
        def body(step, carry):
            for t in range(LINKS):
                place_chunk(k, t, step)
            return carry

        lax.fori_loop(first, SEQS - 1, body, 0)
        for t in range(CHUNKS - LINKS * (SEQS - 1)):
            place_chunk(k, t, SEQS - 1)

    gather(0, 4)
    for t in range(1, LINKS):
        place_chunk(0, t, 3)
    for i in range(1, 8):
        turn(0, i)
    for i in range(1, 4):
        full(0, i, i * W)
    for i in range(3):
        full(0, 4 + i, EDGE + i * W)

    last = 2048 - EDGE

    def cross(k, c):
        @pl.when(outer)
        def _():
            up(k, c).wait_recv()
            pair = jnp.concatenate([w[last:, band(c)], below[k, :, band(c)]], 0)
            mixed = product(matrix(k, 7), pair)
            back[k, :, band(c)] = mixed[EDGE:]
            down(k, c).start()
            w[last:, band(c)] = mixed[:EDGE]

    def lowest(c):
        rows = pl.ds(3 * W, W)
        w[rows, band(c)] = product(matrix(1, 3), w[rows, band(c)])

    def first_again(c):
        @pl.when(inner)
        def _():
            up(0, c).wait_send()
            down(0, c).wait_recv()

        pair = jnp.concatenate([top[0, :, band(c)], w[EDGE:W, band(c)]], 0)
        w[0:W, band(c)] = product(matrix(1, 0), pair)

        @pl.when(inner)
        def _():
            up(1, c).start()

    def store(index, source, rows, columns):
        return pltpu.make_async_copy(source, out_hbm.at[rows, columns], out_sem.at[index])

    def store_last(c):
        return store(c, w.at[pl.ds(last, EDGE), band(c)], pl.ds(last, EDGE), band(c))

    def store_middle():
        rows = pl.ds(EDGE, last - EDGE)
        return pltpu.make_async_copy(w.at[rows], out_hbm.at[rows], out_sem.at[16])

    def store_first(c):
        return store(8 + c, top.at[1, :, band(c)], pl.ds(0, EDGE), band(c))

    def finish(c):
        @pl.when(inner)
        def _():
            down(1, c).wait_recv()

        @pl.when(row == 0)
        def _():
            top[1, :, band(c)] = w[0:EDGE, band(c)]

        store_first(c).start()

    for c in range(4):
        cross(0, c)
    gather(1, 0)
    for i in range(8):
        turn(1, i)
    for i in range(1, 3):
        full(1, i, i * W)
    for c in range(4):
        lowest(c)
    for c in range(2):
        first_again(c)
    for c in range(4, 8):
        cross(0, c)
        lowest(c)
        first_again(c - 2)
    first_again(6)
    cross(1, 0)
    store_last(0).start()
    first_again(7)
    for i in range(3):
        full(1, 4 + i, EDGE + i * W)
    store_middle().start()
    for c in range(1, 8):
        cross(1, c)
        store_last(c).start()
        if c >= 2:
            finish(c - 2)
    finish(6)
    finish(7)

    def settle(step, carry):
        reflect(step).wait_send()
        whole(stage, step, send_sem).wait()
        return carry

    lax.fori_loop(0, STEPS, settle, 0)
    for copy in parts:
        copy.wait_send()
    for c in range(BANDS):
        store_last(c).wait()
        store_first(c).wait()

        @pl.when(inner)
        def _(c=c):
            up(1, c).wait_send()

        @pl.when(outer)
        def _(c=c):
            down(0, c).wait_send()
            down(1, c).wait_send()

    store_middle().wait()


def local(slab, transforms, owners):
    half = (2, G, W)
    rows, columns = slab.shape
    dma = pltpu.SemaphoreType.DMA
    return pl.pallas_call(
        sweep_kernel,
        out_shape=jax.ShapeDtypeStruct(slab.shape, jnp.bfloat16),
        in_specs=[
            pl.BlockSpec(memory_space=pltpu.SMEM),
            pl.BlockSpec(memory_space=pltpu.SMEM),
            pl.BlockSpec(memory_space=pl.ANY),
            pl.BlockSpec(memory_space=pl.ANY),
        ],
        out_specs=pl.BlockSpec(memory_space=pl.ANY),
        scratch_shapes=[
            pltpu.VMEM((CHUNKS,) + half, jnp.bfloat16),
            pltpu.VMEM((CHUNKS,) + half, jnp.bfloat16),
            pltpu.VMEM((STEPS, LINKS) + half, jnp.bfloat16),
            pltpu.VMEM((STEPS, LINKS) + half, jnp.bfloat16),
            pltpu.VMEM((STEPS, LINKS) + half, jnp.bfloat16),
            pltpu.VMEM((2, CHUNKS) + half, jnp.bfloat16),
            pltpu.VMEM((rows, columns), jnp.bfloat16),
            pltpu.VMEM((2, EDGE, columns), jnp.bfloat16),
            pltpu.VMEM((2, EDGE, columns), jnp.bfloat16),
            pltpu.VMEM((2, EDGE, columns), jnp.bfloat16),
            dma((2,)),
            dma((3,)),
            dma((3,)),
            dma((STEPS,)),
            dma((STEPS,)),
            dma((STEPS,)),
            dma((STEPS,)),
            dma((2, BANDS)),
            dma((2, BANDS)),
            dma((2, BANDS)),
            dma((2, BANDS)),
            dma((2 * BANDS + 1,)),
        ],
        compiler_params=pltpu.CompilerParams(
            collective_id=0, has_side_effects=True, vmem_limit_bytes=62 * 1024 * 1024
        ),
        name="sweep",
    )(owners, tree_tables(), transforms[0].reshape((CHUNKS,) + half), slab)


def solution(mesh):
    return jax.shard_map(
        local,
        mesh=mesh,
        in_specs=(P("rows", "cols"), P("cols", "rows", None), P()),
        out_specs=P("rows", "cols"),
        check_vma=False,
    )
```

```python
import functools

import jax
import jax.numpy as jnp
from jax import lax
from jax.experimental import pallas as pl
from jax.experimental.pallas import tpu as pltpu
from jax.sharding import PartitionSpec as P

MESH = pl.DeviceIdType.MESH

PARENT = (
    0, 10234, 10234, 10324, 21034, 40231, 40231, 4321,
    10324, 43102, 40123, 34201, 1423, 30421, 30412, 13042,
    10324, 30124, 42310, 31240, 1342, 21043, 24301, 43102,
    1324, 24310, 42130, 21034, 13042, 40213, 20314, 12430,
)
DEPTH = (
    11111, 13333, 22464, 31555, 53531, 24442, 33553, 62664,
    55133, 44266, 55355, 44646, 44242, 35353, 44466, 53355,
    66224, 55335, 64446, 55555, 55333, 46644, 55555, 64644,
    35313, 26426, 53555, 44464, 66622, 35535, 44646, 53553,
)
OPPOSITE = (1, 0, 3, 2, 4)
LINKS = 5
LAG = 5
CHUNKS = 128
SEQS = 26
STEPS = SEQS + LAG * 5
G = 16
BANDS = 8
BAND = 128
W = 512
EDGE = 256
EARLY = 3 + LAG * 5


def digits(words):
    return [[word // 10 ** (4 - i) % 10 for i in range(5)] for word in words]


def tree_tables():
    parent = digits(PARENT)
    depth = digits(DEPTH)
    forward = []
    for place in range(32):
        y, z, x = place // 8, place // 4 % 2, place % 4
        ahead = (
            (y * 2 + z) * 4 + (x + 1) % 4,
            (y * 2 + z) * 4 + (x + 3) % 4,
            ((y + 1) % 4 * 2 + z) * 4 + x,
            ((y + 3) % 4 * 2 + z) * 4 + x,
            (y * 2 + 1 - z) * 4 + x,
        )
        row = []
        for link in range(LINKS):
            source = 0
            if place and ahead[link]:
                tree = parent[ahead[link]].index(OPPOSITE[link])
                source = parent[place][tree]
            row.append(source)
        forward.append(row)
    flat = []
    for place in range(32):
        flat += forward[place] + parent[place] + [level - 1 for level in depth[place]]
    return jnp.array(flat, jnp.int32)


def sweep_kernel(
    owners, table, slot_hbm, slab_hbm, w,
    own, other, recv, mirror, stage, q, below, top, back,
    load_sem, part_send, part_recv, send_sem, recv_sem, mirror_send, mirror_recv,
    up_send, up_recv, down_send, down_recv,
):
    row = lax.axis_index("rows")
    col = lax.axis_index("cols")
    core = col % 2
    x = (col // 2) % 4
    z = (col // 8) % 2
    y = col // 16

    def device(yy, zz, xx, cc):
        return {"cols": ((yy * 2 + zz) * 4 + xx) * 2 + cc}

    peers = (
        device(y, z, (x + 1) % 4, core),
        device(y, z, (x + 3) % 4, core),
        device((y + 1) % 4, z, x, core),
        device((y + 3) % 4, z, x, core),
        device(y, 1 - z, x, core),
    )
    partner = device(y, z, x, 1 - core)
    upper = {"rows": (row + 3) % 4}
    lower = {"rows": (row + 1) % 4}

    def load(index, first, count):
        rows = pl.ds(first, count)
        return pltpu.make_async_copy(slot_hbm.at[rows], own.at[rows], load_sem.at[index])

    loads = (load(0, 0, 32), load(1, 32, 96))
    load_slab = pltpu.make_async_copy(slab_hbm, w, load_sem.at[2])
    for copy in loads:
        copy.start()
    barrier = pltpu.get_barrier_semaphore()
    for peer in peers + (partner, upper, lower):
        pl.semaphore_signal(barrier, inc=1, device_id=peer, device_id_type=MESH)
    pl.semaphore_wait(barrier, 8)

    def part(index, first, count, half):
        return pltpu.make_async_remote_copy(
            src_ref=slot_hbm.at[pl.ds(first, count), half],
            dst_ref=other.at[pl.ds(first, count), half],
            send_sem=part_send.at[index],
            recv_sem=part_recv.at[index],
            device_id=partner,
            device_id_type=MESH,
        )

    parts = (part(0, 0, 32, 1 - core), part(1, 32, 96, 1 - core), part(2, 0, 128, core))
    for copy in parts[:2]:
        copy.start()

    place, rooted, root_core = [], [], []
    for k in range(2):
        owner = owners[k, row]
        oy, oz, ox, oc = owner // 16, (owner // 8) % 2, (owner // 2) % 4, owner % 2
        where = (((y + 4 - oy) % 4) * 2 + (z + 2 - oz) % 2) * 4 + (x + 4 - ox) % 4
        place.append(where)
        rooted.append(where == 0)
        root_core.append(oc == core)
    source = [[table[place[k] * 15 + l] for l in range(LINKS)] for k in range(2)]
    entry = [[table[place[k] * 15 + 5 + l] for l in range(LINKS)] for k in range(2)]
    level = [[table[place[k] * 15 + 10 + l] for l in range(LINKS)] for k in range(2)]

    def fill(step, local, passed):
        for l in range(LINKS):
            chunk = None
            if local:
                chunk = step * LINKS + l
                if isinstance(chunk, int):
                    chunk = min(chunk, CHUNKS - 1)
                mine, theirs = own[chunk, core], other[chunk, core]
            for k in range(2):
                value = None
                if passed:
                    value = recv[step - LAG, 0, k]
                    for m in range(1, LINKS):
                        value = jnp.where(source[k][l] == m, recv[step - LAG, m, k], value)
                if local:
                    first = jnp.where(root_core[k], mine, theirs)
                    value = first if value is None else jnp.where(rooted[k], first, value)
                stage[step, l, k] = value

    def send(step):
        for l in range(LINKS):
            pltpu.make_async_remote_copy(
                src_ref=stage.at[step, l],
                dst_ref=recv.at[step, OPPOSITE[l]],
                send_sem=send_sem.at[step],
                recv_sem=recv_sem.at[step],
                device_id=peers[l],
                device_id_type=MESH,
            ).start()

    def whole(ref, step, sem):
        return pltpu.make_async_copy(ref.at[step], ref.at[step], sem.at[step])

    def reflect(step):
        return pltpu.make_async_remote_copy(
            src_ref=recv.at[step],
            dst_ref=mirror.at[step],
            send_sem=mirror_send.at[step],
            recv_sem=mirror_recv.at[step],
            device_id=partner,
            device_id_type=MESH,
        )

    def arrive(step):
        whole(recv, step, recv_sem).wait()
        reflect(step).start()

    def pass_on(step, carry):
        arrive(step - LAG)
        fill(step, False, True)
        send(step)
        return carry

    def both(step, carry):
        arrive(step - LAG)
        fill(step, True, True)
        send(step)
        return carry

    def reflected(step, carry):
        reflect(step).wait_recv()
        return carry

    loads[0].wait()
    parts[0].wait_recv()
    for step in range(LAG):
        fill(step, True, False)
        send(step)
    loads[1].wait()
    parts[1].wait_recv()
    parts[2].start()
    load_slab.start()
    lax.fori_loop(LAG, SEQS - 1, both, 0)
    both(SEQS - 1, 0)
    lax.fori_loop(SEQS, EARLY + LAG + 3, pass_on, 0)
    parts[2].wait_recv()
    lax.fori_loop(0, EARLY + 1, reflected, 0)

    def local_rows(k, chunk, half):
        return jnp.where(root_core[k], own[chunk, half], other[chunk, half])

    for chunk in range(W // (2 * G)):
        step, t = chunk // LINKS, chunk % LINKS
        for half, got in ((core, recv), (1 - core, mirror)):
            value = got[step, 0, 0]
            for d in range(6):
                here = got[step + LAG * d, 0, 0]
                for m in range(1, LINKS):
                    here = jnp.where(entry[0][t] == m, got[step + LAG * d, m, 0], here)
                value = jnp.where(level[0][t] == d, here, value)
            q[0, chunk, half] = jnp.where(rooted[0], local_rows(0, chunk, half), value)

    def matrix(k, window):
        return q[k, window * G : (window + 1) * G].reshape(W, W)

    def turn(k, window):
        turned = matrix(k, window).T
        q[k, window * G : (window + 1) * G] = turned.reshape(G, 2, G, W)

    def product(left, right):
        return jnp.dot(left, right, preferred_element_type=jnp.float32).astype(jnp.bfloat16)

    def full(k, window, first):
        rows = pl.ds(first, W)
        w[rows, :] = product(matrix(k, window), w[rows, :])

    def band(c):
        return pl.ds(c * BAND, BAND)

    def up(k, c):
        return pltpu.make_async_remote_copy(
            src_ref=w.at[pl.ds(0, EDGE), band(c)],
            dst_ref=below.at[k, :, band(c)],
            send_sem=up_send.at[k, c],
            recv_sem=up_recv.at[k, c],
            device_id=upper,
            device_id_type=MESH,
        )

    def down(k, c):
        return pltpu.make_async_remote_copy(
            src_ref=back.at[k, :, band(c)],
            dst_ref=top.at[k, :, band(c)],
            send_sem=down_send.at[k, c],
            recv_sem=down_recv.at[k, c],
            device_id=lower,
            device_id_type=MESH,
        )

    inner = row > 0
    outer = row < 3

    load_slab.wait()
    turn(0, 0)
    full(0, 0, 0)

    @pl.when(row == 0)
    def _():
        top[0] = w[0:EDGE, :]

    lax.fori_loop(EARLY + LAG + 3, STEPS, pass_on, 0)

    @pl.when(inner)
    def _():
        for c in range(BANDS):
            up(0, c).start()

    def drain(step, carry):
        arrive(step)
        return carry

    lax.fori_loop(STEPS - LAG, STEPS, drain, 0)
    lax.fori_loop(EARLY + 1, STEPS, reflected, 0)

    def place_chunk(k, t, step):
        chunk = step * LINKS + t
        index = level[k][t] * LAG + step
        for half, got in ((core, recv), (1 - core, mirror)):
            q[k, chunk, half] = jnp.where(
                rooted[k], local_rows(k, chunk, half), got[index, entry[k][t], k]
            )

    def gather(k, first):
        def body(step, carry):
            for t in range(LINKS):
                place_chunk(k, t, step)
            return carry

        lax.fori_loop(first, SEQS - 1, body, 0)
        for t in range(CHUNKS - LINKS * (SEQS - 1)):
            place_chunk(k, t, SEQS - 1)

    gather(0, 4)
    for t in range(1, LINKS):
        place_chunk(0, t, 3)
    for i in range(1, 8):
        turn(0, i)
    for i in range(1, 4):
        full(0, i, i * W)
    for i in range(3):
        full(0, 4 + i, EDGE + i * W)

    last = 2048 - EDGE

    def cross(k, c):
        @pl.when(outer)
        def _():
            up(k, c).wait_recv()
            pair = jnp.concatenate([w[last:, band(c)], below[k, :, band(c)]], 0)
            mixed = product(matrix(k, 7), pair)
            back[k, :, band(c)] = mixed[EDGE:]
            down(k, c).start()
            w[last:, band(c)] = mixed[:EDGE]

    def lowest(first):
        rows, columns = pl.ds(3 * W, W), pl.ds(first * BAND, 4 * BAND)
        w[rows, columns] = product(matrix(1, 3), w[rows, columns])

    def first_again(c):
        @pl.when(inner)
        def _():
            up(0, c).wait_send()
            down(0, c).wait_recv()

        pair = jnp.concatenate([top[0, :, band(c)], w[EDGE:W, band(c)]], 0)
        w[0:W, band(c)] = product(matrix(1, 0), pair)

        @pl.when(inner)
        def _():
            up(1, c).start()

    def finish(c):
        @pl.when(inner)
        def _():
            up(1, c).wait_send()
            down(1, c).wait_recv()
            w[0:EDGE, band(c)] = top[1, :, band(c)]

    for c in range(3):
        cross(0, c)
    gather(1, 0)
    turn(1, 0)
    first_again(0)
    cross(0, 3)
    first_again(1)
    for i in range(1, 4):
        turn(1, i)
    lowest(0)
    cross(0, 4)
    first_again(2)
    full(1, 1, W)
    cross(0, 5)
    first_again(3)
    full(1, 2, 2 * W)
    cross(0, 6)
    first_again(4)
    for i in range(4, 8):
        turn(1, i)
    cross(0, 7)
    first_again(5)
    lowest(4)
    first_again(6)
    cross(1, 0)
    first_again(7)
    for i in range(3):
        full(1, 4 + i, EDGE + i * W)
    for c in range(1, 8):
        cross(1, c)
        if c >= 3:
            finish(c - 3)
    finish(5)
    finish(6)
    finish(7)

    def settle(step, carry):
        reflect(step).wait_send()
        whole(stage, step, send_sem).wait()
        return carry

    lax.fori_loop(0, STEPS, settle, 0)
    for copy in parts:
        copy.wait_send()
    for c in range(BANDS):

        @pl.when(outer)
        def _(c=c):
            down(0, c).wait_send()
            down(1, c).wait_send()


def local(slab, transforms, owners):
    half = (2, G, W)
    rows, columns = slab.shape
    dma = pltpu.SemaphoreType.DMA
    return pl.pallas_call(
        sweep_kernel,
        out_shape=pltpu.VMEM(slab.shape, jnp.bfloat16),
        in_specs=[
            pl.BlockSpec(memory_space=pltpu.SMEM),
            pl.BlockSpec(memory_space=pltpu.SMEM),
            pl.BlockSpec(memory_space=pl.ANY),
            pl.BlockSpec(memory_space=pl.ANY),
        ],
        out_specs=pl.BlockSpec(memory_space=pltpu.VMEM),
        scratch_shapes=[
            pltpu.VMEM((CHUNKS,) + half, jnp.bfloat16),
            pltpu.VMEM((CHUNKS,) + half, jnp.bfloat16),
            pltpu.VMEM((STEPS, LINKS) + half, jnp.bfloat16),
            pltpu.VMEM((STEPS, LINKS) + half, jnp.bfloat16),
            pltpu.VMEM((STEPS, LINKS) + half, jnp.bfloat16),
            pltpu.VMEM((2, CHUNKS) + half, jnp.bfloat16),
            pltpu.VMEM((2, EDGE, columns), jnp.bfloat16),
            pltpu.VMEM((2, EDGE, columns), jnp.bfloat16),
            pltpu.VMEM((2, EDGE, columns), jnp.bfloat16),
            dma((3,)),
            dma((3,)),
            dma((3,)),
            dma((STEPS,)),
            dma((STEPS,)),
            dma((STEPS,)),
            dma((STEPS,)),
            dma((2, BANDS)),
            dma((2, BANDS)),
            dma((2, BANDS)),
            dma((2, BANDS)),
        ],
        compiler_params=pltpu.CompilerParams(
            collective_id=0, has_side_effects=True, vmem_limit_bytes=56 * 1024 * 1024
        ),
        name="sweep",
    )(owners, tree_tables(), transforms[0].reshape((CHUNKS,) + half), slab)


def solution(mesh):
    return jax.shard_map(
        local,
        mesh=mesh,
        in_specs=(P("rows", "cols"), P("cols", "rows", None), P()),
        out_specs=P("rows", "cols"),
        check_vma=False,
    )
```

```python
import functools

import jax
import jax.numpy as jnp
from jax import lax
from jax.experimental import pallas as pl
from jax.experimental.pallas import tpu as pltpu
from jax.sharding import PartitionSpec as P

MESH = pl.DeviceIdType.MESH

PARENT = (
    0, 10234, 10234, 10324, 21034, 40231, 40231, 4321,
    10324, 43102, 40123, 34201, 1423, 30421, 30412, 13042,
    10324, 30124, 42310, 31240, 1342, 21043, 24301, 43102,
    1324, 24310, 42130, 21034, 13042, 40213, 20314, 12430,
)
DEPTH = (
    11111, 13333, 22464, 31555, 53531, 24442, 33553, 62664,
    55133, 44266, 55355, 44646, 44242, 35353, 44466, 53355,
    66224, 55335, 64446, 55555, 55333, 46644, 55555, 64644,
    35313, 26426, 53555, 44464, 66622, 35535, 44646, 53553,
)
OPPOSITE = (1, 0, 3, 2, 4)
LINKS = 5
LAG = 5
CHUNKS = 128
SEQS = 26
STEPS = SEQS + LAG * 5
G = 16
BANDS = 8
BAND = 128
W = 512
EDGE = 256
EARLY = 3 + LAG * 5


def digits(words):
    return [[word // 10 ** (4 - i) % 10 for i in range(5)] for word in words]


def tree_tables():
    parent = digits(PARENT)
    depth = digits(DEPTH)
    forward = []
    for place in range(32):
        y, z, x = place // 8, place // 4 % 2, place % 4
        ahead = (
            (y * 2 + z) * 4 + (x + 1) % 4,
            (y * 2 + z) * 4 + (x + 3) % 4,
            ((y + 1) % 4 * 2 + z) * 4 + x,
            ((y + 3) % 4 * 2 + z) * 4 + x,
            (y * 2 + 1 - z) * 4 + x,
        )
        row = []
        for link in range(LINKS):
            source = 0
            if place and ahead[link]:
                tree = parent[ahead[link]].index(OPPOSITE[link])
                source = parent[place][tree]
            row.append(source)
        forward.append(row)
    flat = []
    for place in range(32):
        flat += forward[place] + parent[place] + [level - 1 for level in depth[place]]
    return jnp.array(flat, jnp.int32)


def reach():
    parent, depth = digits(PARENT), digits(DEPTH)
    trees = []
    for t in range(LINKS):
        seen = {(depth[p][t] - 1, parent[p][t]) for p in range(1, 32)}
        levels = sorted({d for d, _ in seen})
        trees.append([(d, sorted(m for e, m in seen if e == d)) for d in levels])
    return trees


REACH = reach()


def sweep_kernel(
    owners, table, slot_hbm, slab_hbm, w,
    own, other, recv, mirror, stage, q, below, top, back,
    load_sem, part_send, part_recv, send_sem, recv_sem, mirror_send, mirror_recv,
    up_send, up_recv, down_send, down_recv,
):
    row = lax.axis_index("rows")
    col = lax.axis_index("cols")
    core = col % 2
    x = (col // 2) % 4
    z = (col // 8) % 2
    y = col // 16

    def device(yy, zz, xx, cc):
        return {"cols": ((yy * 2 + zz) * 4 + xx) * 2 + cc}

    peers = (
        device(y, z, (x + 1) % 4, core),
        device(y, z, (x + 3) % 4, core),
        device((y + 1) % 4, z, x, core),
        device((y + 3) % 4, z, x, core),
        device(y, 1 - z, x, core),
    )
    partner = device(y, z, x, 1 - core)
    upper = {"rows": (row + 3) % 4}
    lower = {"rows": (row + 1) % 4}

    def load(index, first, count):
        rows = pl.ds(first, count)
        return pltpu.make_async_copy(slot_hbm.at[rows], own.at[rows], load_sem.at[index])

    loads = (load(0, 0, 32), load(1, 32, 96))
    load_slab = pltpu.make_async_copy(slab_hbm, w, load_sem.at[2])
    for copy in loads:
        copy.start()
    barrier = pltpu.get_barrier_semaphore()
    for peer in peers + (partner, upper, lower):
        pl.semaphore_signal(barrier, inc=1, device_id=peer, device_id_type=MESH)
    pl.semaphore_wait(barrier, 8)

    def part(index, first, count, half):
        return pltpu.make_async_remote_copy(
            src_ref=slot_hbm.at[pl.ds(first, count), half],
            dst_ref=other.at[pl.ds(first, count), half],
            send_sem=part_send.at[index],
            recv_sem=part_recv.at[index],
            device_id=partner,
            device_id_type=MESH,
        )

    parts = (part(0, 0, 32, 1 - core), part(1, 32, 96, 1 - core), part(2, 0, 128, core))
    for copy in parts[:2]:
        copy.start()

    place, rooted, root_core = [], [], []
    for k in range(2):
        owner = owners[k, row]
        oy, oz, ox, oc = owner // 16, (owner // 8) % 2, (owner // 2) % 4, owner % 2
        where = (((y + 4 - oy) % 4) * 2 + (z + 2 - oz) % 2) * 4 + (x + 4 - ox) % 4
        place.append(where)
        rooted.append(where == 0)
        root_core.append(oc == core)
    source = [[table[place[k] * 15 + l] for l in range(LINKS)] for k in range(2)]
    entry = [[table[place[k] * 15 + 5 + l] for l in range(LINKS)] for k in range(2)]
    level = [[table[place[k] * 15 + 10 + l] for l in range(LINKS)] for k in range(2)]

    def fill(step, local, passed):
        for l in range(LINKS):
            chunk = None
            if local:
                chunk = step * LINKS + l
                if isinstance(chunk, int):
                    chunk = min(chunk, CHUNKS - 1)
                mine, theirs = own[chunk, core], other[chunk, core]
            for k in range(2):
                value = None
                if passed:
                    value = recv[step - LAG, 0, k]
                    for m in range(1, LINKS):
                        value = jnp.where(source[k][l] == m, recv[step - LAG, m, k], value)
                if local:
                    first = jnp.where(root_core[k], mine, theirs)
                    value = first if value is None else jnp.where(rooted[k], first, value)
                stage[step, l, k] = value

    def send(step):
        for l in range(LINKS):
            pltpu.make_async_remote_copy(
                src_ref=stage.at[step, l],
                dst_ref=recv.at[step, OPPOSITE[l]],
                send_sem=send_sem.at[step],
                recv_sem=recv_sem.at[step],
                device_id=peers[l],
                device_id_type=MESH,
            ).start()

    def whole(ref, step, sem):
        return pltpu.make_async_copy(ref.at[step], ref.at[step], sem.at[step])

    def reflect(step):
        return pltpu.make_async_remote_copy(
            src_ref=recv.at[step],
            dst_ref=mirror.at[step],
            send_sem=mirror_send.at[step],
            recv_sem=mirror_recv.at[step],
            device_id=partner,
            device_id_type=MESH,
        )

    def arrive(step):
        whole(recv, step, recv_sem).wait()
        reflect(step).start()

    def pass_on(step, carry):
        arrive(step - LAG)
        fill(step, False, True)
        send(step)
        return carry

    def both(step, carry):
        arrive(step - LAG)
        fill(step, True, True)
        send(step)
        return carry

    def reflected(step, carry):
        reflect(step).wait_recv()
        return carry

    loads[0].wait()
    parts[0].wait_recv()
    for step in range(LAG):
        fill(step, True, False)
        send(step)
    loads[1].wait()
    parts[1].wait_recv()
    parts[2].start()
    load_slab.start()
    lax.fori_loop(LAG, SEQS - 1, both, 0)
    both(SEQS - 1, 0)
    lax.fori_loop(SEQS, EARLY + LAG + 3, pass_on, 0)
    parts[2].wait_recv()
    lax.fori_loop(0, EARLY + 1, reflected, 0)

    def local_rows(k, chunk, half):
        return jnp.where(root_core[k], own[chunk, half], other[chunk, half])

    for chunk in range(W // (2 * G)):
        step, t = chunk // LINKS, chunk % LINKS
        for half, got in ((core, recv), (1 - core, mirror)):
            value = None
            for d, links in REACH[t]:
                here = got[step + LAG * d, links[0], 0]
                for m in links[1:]:
                    here = jnp.where(entry[0][t] == m, got[step + LAG * d, m, 0], here)
                value = here if value is None else jnp.where(level[0][t] == d, here, value)
            q[0, chunk, half] = jnp.where(rooted[0], local_rows(0, chunk, half), value)

    def matrix(k, window):
        return q[k, window * G : (window + 1) * G].reshape(W, W)

    def turn(k, window):
        turned = matrix(k, window).T
        q[k, window * G : (window + 1) * G] = turned.reshape(G, 2, G, W)

    def product(left, right):
        return jnp.dot(left, right, preferred_element_type=jnp.float32).astype(jnp.bfloat16)

    def full(k, window, first):
        rows = pl.ds(first, W)
        w[rows, :] = product(matrix(k, window), w[rows, :])

    def band(c):
        return pl.ds(c * BAND, BAND)

    def up(k, c):
        return pltpu.make_async_remote_copy(
            src_ref=w.at[pl.ds(0, EDGE), band(c)],
            dst_ref=below.at[k, :, band(c)],
            send_sem=up_send.at[k, c],
            recv_sem=up_recv.at[k, c],
            device_id=upper,
            device_id_type=MESH,
        )

    def down(k, c):
        return pltpu.make_async_remote_copy(
            src_ref=back.at[k, :, band(c)],
            dst_ref=top.at[k, :, band(c)],
            send_sem=down_send.at[k, c],
            recv_sem=down_recv.at[k, c],
            device_id=lower,
            device_id_type=MESH,
        )

    inner = row > 0
    outer = row < 3

    load_slab.wait()
    turn(0, 0)
    full(0, 0, 0)

    @pl.when(row == 0)
    def _():
        top[0] = w[0:EDGE, :]

    lax.fori_loop(EARLY + LAG + 3, STEPS, pass_on, 0)


    def drain(step, carry):
        arrive(step)
        return carry

    lax.fori_loop(STEPS - LAG, STEPS, drain, 0)

    @pl.when(inner)
    def _():
        for c in range(BANDS):
            up(0, c).start()

    lax.fori_loop(EARLY + 1, STEPS, reflected, 0)

    def place_chunk(k, t, step):
        chunk = step * LINKS + t
        index = level[k][t] * LAG + step
        for half, got in ((core, recv), (1 - core, mirror)):
            q[k, chunk, half] = jnp.where(
                rooted[k], local_rows(k, chunk, half), got[index, entry[k][t], k]
            )

    def gather(k, first):
        def body(step, carry):
            for t in range(LINKS):
                place_chunk(k, t, step)
            return carry

        lax.fori_loop(first, SEQS - 1, body, 0)
        for t in range(CHUNKS - LINKS * (SEQS - 1)):
            place_chunk(k, t, SEQS - 1)

    gather(0, 4)
    for t in range(1, LINKS):
        place_chunk(0, t, 3)
    for i in range(1, 8):
        turn(0, i)
    for i in range(1, 4):
        full(0, i, i * W)
    for i in range(3):
        full(0, 4 + i, EDGE + i * W)

    last = 2048 - EDGE

    def cross(k, c):
        @pl.when(outer)
        def _():
            up(k, c).wait_recv()
            pair = jnp.concatenate([w[last:, band(c)], below[k, :, band(c)]], 0)
            mixed = product(matrix(k, 7), pair)
            back[k, :, band(c)] = mixed[EDGE:]
            down(k, c).start()
            w[last:, band(c)] = mixed[:EDGE]

    def lowest(first):
        rows, columns = pl.ds(3 * W, W), pl.ds(first * BAND, 4 * BAND)
        w[rows, columns] = product(matrix(1, 3), w[rows, columns])

    def first_again(c):
        @pl.when(inner)
        def _():
            up(0, c).wait_send()
            down(0, c).wait_recv()

        pair = jnp.concatenate([top[0, :, band(c)], w[EDGE:W, band(c)]], 0)
        w[0:W, band(c)] = product(matrix(1, 0), pair)

        @pl.when(inner)
        def _():
            up(1, c).start()

    def finish(c):
        @pl.when(inner)
        def _():
            up(1, c).wait_send()
            down(1, c).wait_recv()
            w[0:EDGE, band(c)] = top[1, :, band(c)]

    for c in range(3):
        cross(0, c)
    gather(1, 0)
    turn(1, 0)
    first_again(0)
    cross(0, 3)
    first_again(1)
    for i in range(1, 4):
        turn(1, i)
    lowest(0)
    cross(0, 4)
    first_again(2)
    full(1, 1, W)
    cross(0, 5)
    first_again(3)
    full(1, 2, 2 * W)
    cross(0, 6)
    first_again(4)
    for i in range(4, 8):
        turn(1, i)
    cross(0, 7)
    first_again(5)
    lowest(4)
    first_again(6)
    cross(1, 0)
    first_again(7)
    for i in range(3):
        full(1, 4 + i, EDGE + i * W)
    for c in range(1, 8):
        cross(1, c)
        if c >= 3:
            finish(c - 3)
    finish(5)
    finish(6)
    finish(7)

    def settle(step, carry):
        reflect(step).wait_send()
        whole(stage, step, send_sem).wait()
        return carry

    lax.fori_loop(0, STEPS, settle, 0)
    for copy in parts:
        copy.wait_send()
    for c in range(BANDS):

        @pl.when(outer)
        def _(c=c):
            down(0, c).wait_send()
            down(1, c).wait_send()


def local(slab, transforms, owners):
    half = (2, G, W)
    rows, columns = slab.shape
    dma = pltpu.SemaphoreType.DMA
    return pl.pallas_call(
        sweep_kernel,
        out_shape=pltpu.VMEM(slab.shape, jnp.bfloat16),
        in_specs=[
            pl.BlockSpec(memory_space=pltpu.SMEM),
            pl.BlockSpec(memory_space=pltpu.SMEM),
            pl.BlockSpec(memory_space=pl.ANY),
            pl.BlockSpec(memory_space=pl.ANY),
        ],
        out_specs=pl.BlockSpec(memory_space=pltpu.VMEM),
        scratch_shapes=[
            pltpu.VMEM((CHUNKS,) + half, jnp.bfloat16),
            pltpu.VMEM((CHUNKS,) + half, jnp.bfloat16),
            pltpu.VMEM((STEPS, LINKS) + half, jnp.bfloat16),
            pltpu.VMEM((STEPS, LINKS) + half, jnp.bfloat16),
            pltpu.VMEM((STEPS, LINKS) + half, jnp.bfloat16),
            pltpu.VMEM((2, CHUNKS) + half, jnp.bfloat16),
            pltpu.VMEM((2, EDGE, columns), jnp.bfloat16),
            pltpu.VMEM((2, EDGE, columns), jnp.bfloat16),
            pltpu.VMEM((2, EDGE, columns), jnp.bfloat16),
            dma((3,)),
            dma((3,)),
            dma((3,)),
            dma((STEPS,)),
            dma((STEPS,)),
            dma((STEPS,)),
            dma((STEPS,)),
            dma((2, BANDS)),
            dma((2, BANDS)),
            dma((2, BANDS)),
            dma((2, BANDS)),
        ],
        compiler_params=pltpu.CompilerParams(
            collective_id=0, has_side_effects=True, vmem_limit_bytes=56 * 1024 * 1024
        ),
        name="sweep",
    )(owners, tree_tables(), transforms[0].reshape((CHUNKS,) + half), slab)


def solution(mesh):
    return jax.shard_map(
        local,
        mesh=mesh,
        in_specs=(P("rows", "cols"), P("cols", "rows", None), P()),
        out_specs=P("rows", "cols"),
        check_vma=False,
    )
```
